32 devices in a mesh: groups: 2 (over y), tensor: 8 (over z, x), seq: 2 (over core).
Axes of the slice: x: 2, y: 2, z: 4, core: 2. Of those that a mesh axis runs over, the one named last changes fastest.
Arguments:
- stored_hidden: bfloat16 [4, 64, 7168], P(('groups', 'seq'), None, 'tensor'), parts along dimension 0, may hold values from -6 to 6
- w_down_kv: bfloat16 [7168, 576], P('tensor'), may hold values from -0.0625 to 0.0625
- kv_gain: bfloat16 [512], replicated, may hold values from 0.5 to 1.5
- evicted_blocks: int32 [2], P('groups'), parts along dimension 0, may hold values from 0 to 127, as said below
- query_latent: bfloat16 [64, 1536], P(('groups', 'tensor')), parts along dimension 0, may hold values from -6 to 6
- w_up_q: bfloat16 [1536, 24576], P(None, 'tensor'), may hold values from -0.15625 to 0.15625
- w_key_absorb: bfloat16 [128, 128, 512], P('tensor'), may hold values from -0.5 to 0.5
- w_value: bfloat16 [128, 512, 128], P('tensor'), may hold values from -0.25 to 0.25
- query_positions: int32 [64], P('groups'), parts along dimension 0, may hold values from 16384 to 32767
- prefix_lengths: int32 [8], P('groups'), parts along dimension 0, may hold values from 4096 to 16384, as said below
- latent_cache: bfloat16 [32768, 576], P(('groups', 'seq')), parts along dimension 0, may hold values from -500 to 500
Outputs:
- rebuilt: bfloat16 [4, 64, 576], P(('groups', 'seq'), 'tensor'), parts along dimension 0
- attended: bfloat16 [64, 16384], P('groups', 'tensor'), parts along dimension 0
The draws below stay inside these ranges and needn't reach their ends.
There are 2 independent parts, one for each index of `groups`. The reference program is written for one: setup_inputs(seed, part) draws one part's arguments, and reference() takes and returns one part's arrays. A program takes and returns all parts, laid end to end along the dimension named above; an argument that names none is the same for every part. Nothing has to cross between parts.
Inputs may be any that keep to these rules, and one draw needn't show every extreme that they name: `evicted_blocks`: distinct block numbers of the cached prefix. `prefix_lengths`: one request's length is exactly 16384.
All inputs are finite; a program needn't handle non-finite values.
Results may differ from the reference program's by a relative error of at most 0.012.
The reference program's roundings to bfloat16 on the way count: a program that leaves them out, or rounds other values in their place, can miss the bound.
Values may be sent and summed in bfloat16 or wider, within the bound.
A program may use at most 64 MiB of HBM per device.

```python
import jax
import jax.numpy as jnp
from jax import lax

D = 7168
KV_RANK = 512
QL = 1536
H = 128
NOPE = 128
VH = 128
BLK = 128
REQUESTS = 4
E_HALF = 64
EVICTED = 128
S = 16384
Q = 32
C = 576
QK = 192
N_SEQ = 2


def draw_evicted_blocks(key, part):
    block_total = S // BLK
    shuffled = jax.random.permutation(key, block_total)
    chosen = shuffled[:EVICTED // BLK]
    return ((chosen - chosen[0] + block_total - 1) % block_total).astype(jnp.int32)


def draw_prefix_lengths(key, part):
    values_drawn = jax.random.randint(key, (REQUESTS,), S // 4, S + 1)
    picked = jax.random.permutation(jax.random.fold_in(key, 7), REQUESTS)
    return values_drawn.at[picked[0]].set(S).at[picked[1]].set(S // 4).astype(jnp.int32)


def draw_latent_cache(key, part):
    drawn_cache = jax.random.normal(key, (S, C), jnp.float32)
    return drawn_cache.astype(jnp.bfloat16)


def touch_ends(array, own_key, low, top_value):
    longest = array.shape.index(max(array.shape))
    spots = []
    for shift in (0, 1):
        where = [jax.random.randint(jax.random.fold_in(own_key, axis), (), 0, length) for axis, length in enumerate(array.shape)]
        where[longest] = (where[longest] + shift) % array.shape[longest]
        spots.append(tuple(where))
    return array.at[spots[0]].set(low).at[spots[1]].set(top_value)


def spiked(values, own_key, source, target, parts, factor):
    owner, partner = [(jnp.arange(values.shape[axis_at]) // (values.shape[axis_at] // parts)).reshape([-1 if axis == axis_at else 1 for axis in range(values.ndim)]) for axis_at in (source, target)]
    chosen = jax.random.permutation(own_key, parts)[partner]
    strong = (owner == chosen) | (owner == (partner + parts // 2) % parts)
    return jnp.where(strong, factor * values, values)


def levels(stream_key, dims, cuts, low, top_value):
    loudness = 1.0
    for dim, parts in cuts:
        heights = jax.random.uniform(jax.random.fold_in(jax.random.fold_in(stream_key, 6), dim), (parts,), jnp.float32, low / len(cuts), top_value / len(cuts))
        loudness = loudness * jnp.repeat(jnp.exp(heights), dims[dim] // parts).reshape((-1,) + (1,) * (len(dims) - 1 - dim))
    return loudness


def scatter_about(own_key, dims, width, most, cuts=(), held_as=jnp.bfloat16):
    result = width * jax.random.normal(own_key, dims, jnp.float32)
    if cuts:
        result = result * levels(own_key, dims, cuts, -0.22, 0.18)
    return jnp.clip(result, -most, most).astype(held_as)


def bell_draw_with(own_key, extent, width, most, cuts, heavy, held_as=jnp.bfloat16):
    result = width * jax.random.normal(own_key, extent, jnp.float32)
    if cuts:
        result = result * levels(own_key, extent, cuts, -0.22, 0.18)
    return jnp.clip(spiked(result, jax.random.fold_in(own_key, 3), *heavy), -most, most).astype(held_as)


def setup_inputs(seed: int = 0, part: int = 0) -> dict:
    splits = jax.random.split(jax.random.key(seed), 12)
    part_splits = jax.random.split(jax.random.fold_in(splits[11], part), 12)
    stored_hidden = bell_draw_with(part_splits[0], (N_SEQ, E_HALF, D), 1.0, 6.0, ((0, 2), (2, 8)), (2, 1, 8, 2.0))
    w_down_kv = scatter_about(splits[1], (D, C), D ** -0.5, 0.0625, ((0, 8),))
    kv_gain = jnp.clip(1.0 + 0.1 * jax.random.normal(splits[2], (KV_RANK,), jnp.float32), 0.5, 1.5).astype(jnp.bfloat16)
    evicted_blocks = draw_evicted_blocks(jax.random.fold_in(jax.random.fold_in(splits[11], part), 71), part)
    query_latent = scatter_about(part_splits[4], (Q, QL), 1.0, 6.0, ((0, 8),))
    w_up_q = scatter_about(splits[5], (QL, H * QK), QL ** -0.5, 0.15625, ((1, 8),))
    w_key_absorb = scatter_about(splits[6], (H, NOPE, KV_RANK), NOPE ** -0.5, 0.5, ((0, 8),))
    w_value = scatter_about(splits[7], (H, KV_RANK, VH), KV_RANK ** -0.5, 0.25, ((0, 8),))
    query_positions = touch_ends(jax.random.randint(part_splits[8], (Q,), S, 2 * S), jax.random.fold_in(part_splits[8], 1), S, (2 * S) - 1).astype(jnp.int32)
    prefix_lengths = draw_prefix_lengths(jax.random.fold_in(jax.random.fold_in(splits[11], part), 71), part)
    latent_cache = draw_latent_cache(jax.random.fold_in(jax.random.fold_in(splits[11], part), 71), part)
    return dict(stored_hidden=stored_hidden, w_down_kv=w_down_kv, kv_gain=kv_gain, evicted_blocks=evicted_blocks, query_latent=query_latent, w_up_q=w_up_q, w_key_absorb=w_key_absorb, w_value=w_value, query_positions=query_positions, prefix_lengths=prefix_lengths, latent_cache=latent_cache)


def rotate(values, positions):
    half_dim = values.shape[-1] // 2
    freqs = 10000.0 ** (jnp.arange(half_dim, dtype=jnp.float32) * (-2.0 / values.shape[-1]))
    angle = positions.astype(jnp.float32)[..., None] * freqs
    cosine = jnp.cos(angle)
    sine = jnp.sin(angle)
    first = values[..., :half_dim]
    second = values[..., half_dim:]
    return jnp.concatenate([first * cosine - second * sine, second * cosine + first * sine], axis=-1)

def reference(stored_hidden, w_down_kv, kv_gain, evicted_blocks, query_latent, w_up_q, w_key_absorb, w_value, query_positions, prefix_lengths, latent_cache):
    flat_hidden = stored_hidden.reshape(EVICTED, D)
    latent_raw = jnp.dot(flat_hidden, w_down_kv, preferred_element_type=jnp.float32)
    latent = latent_raw[:, :KV_RANK]
    mean_square = lax.optimization_barrier(jnp.mean(latent * latent, axis=-1, keepdims=True))
    normed = latent / jnp.sqrt(mean_square + 1e-06) * kv_gain.astype(jnp.float32)
    flat_index = jnp.arange(EVICTED, dtype=jnp.int32)
    key_position = (evicted_blocks[flat_index // BLK] * BLK + flat_index % BLK).astype(jnp.int32)
    rebuilt_flat = jnp.concatenate([normed, rotate(latent_raw[:, KV_RANK:], key_position)], axis=-1).astype(jnp.bfloat16)
    query_proj = jnp.dot(query_latent, w_up_q, preferred_element_type=jnp.float32).reshape(Q, H, QK)
    query_nope = query_proj[..., :NOPE].astype(jnp.bfloat16)
    absorbed = jnp.einsum('qhn,hnc->qhc', query_nope.astype(jnp.float32), w_key_absorb.astype(jnp.float32))
    rotated = rotate(query_proj[..., NOPE:], query_positions[:, None])
    query_full = (jnp.concatenate([absorbed, rotated], axis=-1) * QK ** (-0.5)).astype(jnp.bfloat16)
    cache_position = jnp.arange(S, dtype=jnp.int32)
    stale = jnp.any((cache_position // BLK)[:, None] == evicted_blocks[None, :], axis=1)
    keys_all = jnp.concatenate([latent_cache, rebuilt_flat], axis=0)
    keys_turned = keys_all.T
    values_all = keys_all[:, :KV_RANK]
    positions_all = jnp.concatenate([cache_position, key_position], axis=0)
    valid_all = jnp.concatenate([jnp.logical_not(stale), jnp.ones((EVICTED,), dtype=jnp.bool_)], axis=0)
    request_of = jnp.arange(Q, dtype=jnp.int32) // (Q // REQUESTS)
    limit = prefix_lengths[request_of]
    allowed = valid_all[None, :] & (positions_all[None, :] < limit[:, None])

    def one_head(pair):
        query_head, value_head = pair
        scores = jnp.dot(query_head, keys_turned, preferred_element_type=jnp.float32)
        largest = lax.optimization_barrier(jnp.max(jnp.where(allowed, scores, -1e+30), axis=-1, keepdims=True))
        prob = jnp.where(allowed, jnp.exp(scores - largest), 0.0)
        denom = lax.optimization_barrier(jnp.sum(prob, axis=-1, keepdims=True))
        latent_out = jnp.dot(prob.astype(jnp.bfloat16), values_all, preferred_element_type=jnp.float32) / denom
        return jnp.dot(latent_out, value_head.astype(jnp.float32), precision=lax.Precision.HIGHEST).astype(jnp.bfloat16)
    outputs = lax.map(one_head, (jnp.transpose(query_full, (1, 0, 2)), w_value))
    attended = jnp.transpose(outputs, (1, 0, 2)).reshape(Q, H * VH)
    rebuilt = rebuilt_flat.reshape(N_SEQ, E_HALF, C)
    return (rebuilt, attended)
```

```python
import functools
import numpy as np
import jax
import jax.numpy as jnp
from jax import lax
from jax.experimental import pallas as pl
from jax.experimental.pallas import tpu as pltpu
from jax.sharding import PartitionSpec as P

BLK = 128
NEG = -1e30
FLOOR = -1e20
FAR = 2**30
NORM_EPS = 1e-06
F32 = jnp.float32
BF16 = jnp.bfloat16
MESH = pl.DeviceIdType.MESH


def swap_halves(x):
    half = x.shape[-1] // 2
    return jnp.concatenate([x[:, half:], x[:, :half]], axis=-1)


def trig(pos, freq, rope_dim):
    angle = pos.astype(F32) * freq
    lane = lax.broadcasted_iota(jnp.int32, angle.shape, 1)
    sine = jnp.sin(angle)
    return jnp.cos(angle), jnp.where(lane < rope_dim // 2, -sine, sine)


def kernel(
    cfg,
    eb_ref, qp_ref, pf_ref, freq_ref, gain_ref,
    hid_hbm, wd_hbm, ql_hbm, wq_hbm, wk_hbm, wv_hbm, kc_hbm,
    reb_ref, att_ref,
    hid, wd, ql, qlf, wq, wk, wv, kc,
    qf, part, rsum, rown, rall, m_s, l_s, acc_s, lim_s, osend, orecv,
    w_sem, q_sem, c_sem, ql_ss, ql_rs, rs_ss, rs_rs, ag_ss, ag_rs, ex_ss, ex_rs,
):
    T, heads, nope, rank, rope_dim, Q, requests, nq, nb, bk, ng = cfg
    me = lax.axis_index("tensor")
    sq = lax.axis_index("seq")
    other = 1 - sq
    head_qk = nope + rope_dim
    piece = ql_hbm.shape[0]
    half_rows = hid.shape[0]
    local = half_rows // T
    R = heads * Q
    n_evicted = eb_ref.shape[0]
    hq = heads // nq

    def far(d):
        return lax.rem(me + d, T)

    def near(d):
        return lax.rem(me + T - d, T)

    barrier = pltpu.get_barrier_semaphore()
    for d in range(1, T):
        pl.semaphore_signal(barrier, inc=1, device_id={"tensor": far(d)}, device_id_type=MESH)
    pl.semaphore_signal(barrier, inc=1, device_id={"seq": other}, device_id_type=MESH)

    own_q = pltpu.make_async_copy(ql_hbm, ql.at[me], w_sem.at[0])
    c_hid = pltpu.make_async_copy(hid_hbm.at[0], hid, w_sem.at[1])
    c_wd = pltpu.make_async_copy(wd_hbm, wd, w_sem.at[2])
    c_wk = pltpu.make_async_copy(wk_hbm, wk, w_sem.at[3])
    c_wv = pltpu.make_async_copy(wv_hbm, wv, w_sem.at[4])
    wide = hq * head_qk
    c_wq = [
        pltpu.make_async_copy(
            wq_hbm.at[:, pl.ds(i * wide, wide)], wq.at[:, pl.ds(i * wide, wide)], q_sem.at[i]
        )
        for i in range(nq)
    ]

    def c_kc(i):
        cols = pl.ds(pl.multiple_of(i * bk, bk), bk)
        return pltpu.make_async_copy(kc_hbm.at[:, cols], kc.at[i], c_sem.at[i])

    own_q.start()
    c_hid.start()
    c_wd.start()
    for c in c_wq:
        c.start()
    c_wk.start()
    for i in range(nb):
        c_kc(i).start()
    c_wv.start()

    freq = freq_ref[...]
    qrow = lax.broadcasted_iota(jnp.int32, (Q, 1), 0)
    qpos = lax.fori_loop(
        0, Q, lambda i, v: jnp.where(qrow == i, qp_ref[i], v), jnp.zeros((Q, 1), jnp.int32)
    )
    qcos, qsin = trig(qpos, freq, rope_dim)
    per = Q // requests
    limit = jnp.zeros((Q, 1), jnp.int32)
    for r in range(requests):
        limit = jnp.where((qrow >= r * per) & (qrow < (r + 1) * per), pf_ref[r], limit)
    for h in range(heads):
        lim_s[h * Q:(h + 1) * Q, :] = limit
    m_s[...] = jnp.full(m_s.shape, FLOOR, F32)
    l_s[...] = jnp.zeros(l_s.shape, F32)
    acc_s[...] = jnp.zeros(acc_s.shape, F32)
    flat0 = sq * half_rows + me * local
    rpos = (
        eb_ref[flat0 // BLK] * BLK + flat0 % BLK
        + lax.broadcasted_iota(jnp.int32, (local, 1), 0)
    )
    rcos, rsin = trig(rpos, freq, rope_dim)

    pl.semaphore_wait(barrier, T)

    def ql_copy(d, slot):
        return pltpu.make_async_remote_copy(
            src_ref=ql_hbm, dst_ref=ql.at[slot], send_sem=ql_ss.at[d], recv_sem=ql_rs.at[d],
            device_id={"tensor": far(d)}, device_id_type=MESH,
        )

    def rs_copy(d, slot):
        return pltpu.make_async_remote_copy(
            src_ref=part.at[far(d)], dst_ref=rsum.at[slot], send_sem=rs_ss.at[d],
            recv_sem=rs_rs.at[d], device_id={"tensor": far(d)}, device_id_type=MESH,
        )

    def ag_copy(d, slot):
        return pltpu.make_async_remote_copy(
            src_ref=rown, dst_ref=rall.at[slot], send_sem=ag_ss.at[d], recv_sem=ag_rs.at[d],
            device_id={"tensor": far(d)}, device_id_type=MESH,
        )

    for d in range(1, T):
        ql_copy(d, me).start()

    c_hid.wait()
    c_wd.wait()
    partial = lax.dot_general(
        hid[...], wd[...], (((1,), (1,)), ((), ())), preferred_element_type=F32
    )
    for t in range(T):
        part[t] = partial[t * local:(t + 1) * local, :]
    rsum[me] = part[me]
    for d in range(1, T):
        rs_copy(d, me).start()

    own_q.wait()
    for d in range(1, T):
        ql_copy(d, near(d)).wait_recv()
    for t in range(T):
        qlf[t * piece:(t + 1) * piece, :] = ql[t].astype(F32)
    queries = qlf[...].astype(BF16)
    scale = float(head_qk) ** (-0.5)
    for i in range(nq):
        c_wq[i].wait()
        if i == 0:
            c_wk.wait()
        proj = jnp.dot(
            queries, wq[:, i * wide:(i + 1) * wide], preferred_element_type=F32
        )
        for j in range(hq):
            h = i * hq + j
            q_nope = proj[:, j * head_qk:j * head_qk + nope].astype(BF16)
            q_rope = proj[:, j * head_qk + nope:(j + 1) * head_qk]
            absorbed = jnp.dot(q_nope, wk[h], preferred_element_type=F32)
            qf[h * Q:(h + 1) * Q, :rank] = (absorbed * scale).astype(BF16)
            turned = q_rope * qcos + swap_halves(q_rope) * qsin
            qf[h * Q:(h + 1) * Q, rank:] = (turned * scale).astype(BF16)

    for d in range(1, T):
        rs_copy(d, near(d)).wait_recv()
    summed = rsum[0]
    for t in range(1, T):
        summed = summed + rsum[t]
    latent = summed[:, :rank]
    mean_square = jnp.mean(latent * latent, axis=-1, keepdims=True)
    normed = latent / jnp.sqrt(mean_square + NORM_EPS) * gain_ref[...].astype(F32).reshape(1, rank)
    tail = summed[:, rank:]
    turned = tail * rcos + swap_halves(tail) * rsin
    rown[:, :rank] = normed.astype(BF16)
    rown[:, rank:] = turned.astype(BF16)
    reb_ref[0] = rown[...]
    rall[me] = rown[...]
    for d in range(1, T):
        ag_copy(d, me).start()

    halves = 2
    rr = R // halves

    def attend(keys, pos, key_dim):
        values = keys[:rank, :] if key_dim else keys[:, :rank]
        for g in range(halves):
            rows = pl.ds(g * rr, rr)
            s = lax.dot_general(
                qf[rows, :], keys, (((1,), (1 - key_dim,)), ((), ())), preferred_element_type=F32
            )
            s = jnp.where(pos < lim_s[rows, :], s, NEG)
            m_old = m_s[rows, :]
            m_new = jnp.maximum(m_old, jnp.max(s, axis=1, keepdims=True))
            p = jnp.exp(s - m_new)
            alpha = jnp.exp(m_old - m_new)
            m_s[rows, :] = m_new
            l_s[rows, :] = l_s[rows, :] * alpha + jnp.sum(p, axis=1, keepdims=True)
            acc_s[rows, :] = acc_s[rows, :] * alpha + lax.dot_general(
                p.astype(BF16), values, (((1,), (key_dim,)), ((), ())),
                preferred_element_type=F32,
            )

    def step(i, carry):
        c_kc(i).wait()
        pos = sq * (nb * bk) + i * bk + lax.broadcasted_iota(jnp.int32, (1, bk), 1)
        eff = pos
        for e in range(n_evicted):
            first = eb_ref[e] * BLK
            eff = jnp.where((pos >= first) & (pos < first + BLK), FAR, eff)
        attend(kc[i], eff, 1)
        return carry

    lax.fori_loop(0, nb, step, 0)

    for d in range(1, T):
        ag_copy(d, near(d)).wait_recv()
    fresh = jnp.concatenate([rall[t].astype(F32) for t in range(T)], axis=0).astype(BF16)
    flat = sq * half_rows + lax.broadcasted_iota(jnp.int32, (1, half_rows), 1)
    fpos = flat
    for e in range(n_evicted):
        inside = (flat >= e * BLK) & (flat < (e + 1) * BLK)
        fpos = jnp.where(inside, eb_ref[e] * BLK + flat - e * BLK, fpos)
    attend(fresh, fpos, 0)

    vh = wv.shape[2]
    gcols = (heads // ng) * vh

    def ex_copy(g):
        cols = pl.ds(g * gcols, gcols) if g < ng else pl.ds(heads * vh, 128)
        return pltpu.make_async_remote_copy(
            src_ref=osend.at[:, cols], dst_ref=orecv.at[:, cols], send_sem=ex_ss.at[g],
            recv_sem=ex_rs.at[g], device_id={"seq": other}, device_id_type=MESH,
        )

    lane = lax.broadcasted_iota(jnp.int32, (Q, 128), 1)
    stats = jnp.zeros((Q, 128), F32)
    for h in range(heads):
        stats = jnp.where(lane == h, m_s[h * Q:(h + 1) * Q, :], stats)
        stats = jnp.where(lane == heads + h, l_s[h * Q:(h + 1) * Q, :], stats)
    osend[:, heads * vh:] = stats
    ex_copy(ng).start()
    c_wv.wait()
    for g in range(ng):
        for h in range(g * (heads // ng), (g + 1) * (heads // ng)):
            a = acc_s[h * Q:(h + 1) * Q, :]
            high = a.astype(BF16)
            low = (a - high.astype(F32)).astype(BF16)
            both = jnp.dot(
                jnp.concatenate([high, low], axis=0), wv[h], preferred_element_type=F32
            )
            osend[:, h * vh:(h + 1) * vh] = both[:Q] + both[Q:]
        ex_copy(g).start()

    ex_copy(ng).wait_recv()
    theirs = orecv[:, heads * vh:]
    m_a, m_b = stats[:, :heads], theirs[:, :heads]
    joint = jnp.maximum(m_a, m_b)
    e_a, e_b = jnp.exp(m_a - joint), jnp.exp(m_b - joint)
    total = e_a * stats[:, heads:2 * heads] + e_b * theirs[:, heads:2 * heads]
    e_a, e_b = e_a / total, e_b / total
    for g in range(ng):
        ex_copy(g).wait_recv()
        for h in range(g * (heads // ng), (g + 1) * (heads // ng)):
            cols = slice(h * vh, (h + 1) * vh)
            att_ref[:, cols] = (
                e_a[:, h:h + 1] * osend[:, cols] + e_b[:, h:h + 1] * orecv[:, cols]
            ).astype(BF16)

    for d in range(1, T):
        ql_copy(d, me).wait_send()
        rs_copy(d, me).wait_send()
        ag_copy(d, me).wait_send()
    for g in range(ng + 1):
        ex_copy(g).wait_send()


def body(
    stored_hidden, w_down_kv, kv_gain, evicted_blocks, query_latent, w_up_q,
    w_key_absorb, w_value, query_positions, prefix_lengths, latent_cache,
):
    T = lax.axis_size("tensor")
    rank = kv_gain.shape[0]
    heads, nope = w_key_absorb.shape[:2]
    width = w_down_kv.shape[1]
    rope_dim = width - rank
    Q = query_positions.shape[0]
    requests = prefix_lengths.shape[0]
    half_rows = stored_hidden.shape[1]
    local = half_rows // T
    cache_rows = latent_cache.shape[0]
    bk = min(1024, cache_rows)
    nb = cache_rows // bk
    nq = max(1, heads // 4)
    ng = max(1, heads // 4)
    vh = w_value.shape[2]
    R = heads * Q
    half = np.arange(rope_dim // 2, dtype=np.float64) * (-2.0 / rope_dim)
    freq = jnp.asarray(np.tile(10000.0 ** half, 2)[None, :].astype(np.float32))
    cfg = (T, heads, nope, rank, rope_dim, Q, requests, nq, nb, bk, ng)
    smem = pl.BlockSpec(memory_space=pltpu.SMEM)
    vmem = pl.BlockSpec(memory_space=pltpu.VMEM)
    hbm = pl.BlockSpec(memory_space=pl.ANY)
    dma = pltpu.SemaphoreType.DMA
    return pl.pallas_call(
        functools.partial(kernel, cfg),
        name="rebuild_attend",
        out_shape=(
            jax.ShapeDtypeStruct((1, local, width), BF16),
            jax.ShapeDtypeStruct((Q, heads * vh), BF16),
        ),
        in_specs=[smem] * 3 + [vmem] * 2 + [hbm] * 7,
        out_specs=(vmem, vmem),
        scratch_shapes=[
            pltpu.VMEM((half_rows, w_down_kv.shape[0]), BF16),
            pltpu.VMEM(w_down_kv.shape[::-1], BF16),
            pltpu.VMEM((T,) + query_latent.shape, BF16),
            pltpu.VMEM((Q, query_latent.shape[1]), F32),
            pltpu.VMEM(w_up_q.shape, BF16),
            pltpu.VMEM(w_key_absorb.shape, BF16),
            pltpu.VMEM(w_value.shape, BF16),
            pltpu.VMEM((nb, width, bk), BF16),
            pltpu.VMEM((R, width), BF16),
            pltpu.VMEM((T, local, width), F32),
            pltpu.VMEM((T, local, width), F32),
            pltpu.VMEM((local, width), BF16),
            pltpu.VMEM((T, local, width), BF16),
            pltpu.VMEM((R, 1), F32),
            pltpu.VMEM((R, 1), F32),
            pltpu.VMEM((R, rank), F32),
            pltpu.VMEM((R, 1), jnp.int32),
            pltpu.VMEM((Q, heads * vh + 128), F32),
            pltpu.VMEM((Q, heads * vh + 128), F32),
            dma((5,)), dma((nq,)), dma((nb,)),
            dma((T,)), dma((T,)), dma((T,)), dma((T,)), dma((T,)), dma((T,)),
            dma((ng + 1,)), dma((ng + 1,)),
        ],
        compiler_params=pltpu.CompilerParams(
            collective_id=0, has_side_effects=True, vmem_limit_bytes=60 * 1024 * 1024
        ),
    )(
        evicted_blocks, query_positions, prefix_lengths, freq, kv_gain,
        stored_hidden, w_down_kv.T, query_latent, w_up_q, w_key_absorb, w_value, latent_cache.T,
    )


def solution(mesh):
    placed = (
        P(("groups", "seq"), None, "tensor"),
        P("tensor", None),
        P(),
        P("groups"),
        P(("groups", "tensor"), None),
        P(None, "tensor"),
        P("tensor", None, None),
        P("tensor", None, None),
        P("groups"),
        P("groups"),
        P(("groups", "seq"), None),
    )
    return jax.shard_map(
        body,
        mesh=mesh,
        in_specs=placed,
        out_specs=(P(("groups", "seq"), "tensor", None), P("groups", "tensor")),
        check_vma=False,
    )
```

```python
import functools
import numpy as np
import jax
import jax.numpy as jnp
from jax import lax
from jax.experimental import pallas as pl
from jax.experimental.pallas import tpu as pltpu
from jax.sharding import PartitionSpec as P

BLK = 128
NEG = -1e30
FLOOR = -1e20
FAR = 2**30
NORM_EPS = 1e-06
F32 = jnp.float32
BF16 = jnp.bfloat16
MESH = pl.DeviceIdType.MESH


def swap_halves(x):
    half = x.shape[-1] // 2
    return jnp.concatenate([x[:, half:], x[:, :half]], axis=-1)


def trig(pos, freq, rope_dim):
    angle = pos.astype(F32) * freq
    lane = lax.broadcasted_iota(jnp.int32, angle.shape, 1)
    sine = jnp.sin(angle)
    return jnp.cos(angle), jnp.where(lane < rope_dim // 2, -sine, sine)


def kernel(
    cfg,
    eb_ref, qp_ref, pf_ref, freq_ref, gain_ref,
    hid_hbm, wd_hbm, ql_hbm, wq_hbm, wk_hbm, wv_hbm, kc_hbm,
    reb_ref, att_ref,
    hid, wd, ql, qlf, wq, wk, wv, kc,
    qf, part, rsum, rown, rall, m_s, l_s, acc_s, lim_s, osend, orecv,
    w_sem, q_sem, c_sem, ql_ss, ql_rs, rs_ss, rs_rs, ag_ss, ag_rs, ex_ss, ex_rs,
):
    T, heads, nope, rank, rope_dim, Q, requests, nq, nb, bk, ng = cfg
    me = lax.axis_index("tensor")
    sq = lax.axis_index("seq")
    other = 1 - sq
    head_qk = nope + rope_dim
    piece = ql_hbm.shape[0]
    half_rows = hid.shape[0]
    local = half_rows // T
    R = heads * Q
    n_evicted = eb_ref.shape[0]
    hq = heads // nq

    def far(d):
        return lax.rem(me + d, T)

    def near(d):
        return lax.rem(me + T - d, T)

    barrier = pltpu.get_barrier_semaphore()
    for d in range(1, T):
        pl.semaphore_signal(barrier, inc=1, device_id={"tensor": far(d)}, device_id_type=MESH)
    pl.semaphore_signal(barrier, inc=1, device_id={"seq": other}, device_id_type=MESH)

    own_q = pltpu.make_async_copy(ql_hbm, ql.at[me], w_sem.at[0])
    c_hid = pltpu.make_async_copy(hid_hbm.at[0], hid, w_sem.at[1])
    c_wd = pltpu.make_async_copy(wd_hbm, wd, w_sem.at[2])
    c_wk = pltpu.make_async_copy(wk_hbm, wk, w_sem.at[3])
    c_wv = pltpu.make_async_copy(wv_hbm, wv, w_sem.at[4])
    wide = hq * head_qk
    c_wq = [
        pltpu.make_async_copy(
            wq_hbm.at[:, pl.ds(i * wide, wide)], wq.at[:, pl.ds(i * wide, wide)], q_sem.at[i]
        )
        for i in range(nq)
    ]

    def c_kc(i):
        cols = pl.ds(pl.multiple_of(i * bk, bk), bk)
        return pltpu.make_async_copy(kc_hbm.at[:, cols], kc.at[i], c_sem.at[i])

    own_q.start()
    c_hid.start()
    c_wd.start()
    for c in c_wq:
        c.start()
    c_wk.start()
    for i in range(nb):
        c_kc(i).start()
    c_wv.start()

    freq = freq_ref[...]
    qrow = lax.broadcasted_iota(jnp.int32, (Q, 1), 0)
    qpos = lax.fori_loop(
        0, Q, lambda i, v: jnp.where(qrow == i, qp_ref[i], v), jnp.zeros((Q, 1), jnp.int32)
    )
    qcos, qsin = trig(qpos, freq, rope_dim)
    per = Q // requests
    limit = jnp.zeros((Q, 1), jnp.int32)
    for r in range(requests):
        limit = jnp.where((qrow >= r * per) & (qrow < (r + 1) * per), pf_ref[r], limit)
    for h in range(heads):
        lim_s[h * Q:(h + 1) * Q, :] = limit
    m_s[...] = jnp.full(m_s.shape, FLOOR, F32)
    l_s[...] = jnp.zeros(l_s.shape, F32)
    acc_s[...] = jnp.zeros(acc_s.shape, F32)
    flat0 = sq * half_rows + me * local
    rpos = (
        eb_ref[flat0 // BLK] * BLK + flat0 % BLK
        + lax.broadcasted_iota(jnp.int32, (local, 1), 0)
    )
    rcos, rsin = trig(rpos, freq, rope_dim)

    pl.semaphore_wait(barrier, T)

    def ql_copy(d, slot):
        return pltpu.make_async_remote_copy(
            src_ref=ql_hbm, dst_ref=ql.at[slot], send_sem=ql_ss.at[d], recv_sem=ql_rs.at[d],
            device_id={"tensor": far(d)}, device_id_type=MESH,
        )

    def rs_copy(d, slot):
        return pltpu.make_async_remote_copy(
            src_ref=part.at[far(d)], dst_ref=rsum.at[slot], send_sem=rs_ss.at[d],
            recv_sem=rs_rs.at[d], device_id={"tensor": far(d)}, device_id_type=MESH,
        )

    def ag_copy(d, slot):
        return pltpu.make_async_remote_copy(
            src_ref=rown, dst_ref=rall.at[slot], send_sem=ag_ss.at[d], recv_sem=ag_rs.at[d],
            device_id={"tensor": far(d)}, device_id_type=MESH,
        )

    for d in range(1, T):
        ql_copy(d, me).start()

    c_hid.wait()
    c_wd.wait()
    partial = lax.dot_general(
        hid[...], wd[...], (((1,), (1,)), ((), ())), preferred_element_type=F32
    )
    for t in range(T):
        part[t] = partial[t * local:(t + 1) * local, :]
    rsum[me] = part[me]
    for d in range(1, T):
        rs_copy(d, me).start()

    own_q.wait()
    for d in range(1, T):
        ql_copy(d, near(d)).wait_recv()
    for t in range(T):
        qlf[t * piece:(t + 1) * piece, :] = ql[t].astype(F32)
    queries = qlf[...].astype(BF16)
    scale = float(head_qk) ** (-0.5)
    for i in range(nq):
        c_wq[i].wait()
        if i == 0:
            c_wk.wait()
        proj = jnp.dot(
            queries, wq[:, i * wide:(i + 1) * wide], preferred_element_type=F32
        )
        for j in range(hq):
            h = i * hq + j
            q_nope = proj[:, j * head_qk:j * head_qk + nope].astype(BF16)
            q_rope = proj[:, j * head_qk + nope:(j + 1) * head_qk]
            absorbed = jnp.dot(q_nope, wk[h], preferred_element_type=F32)
            qf[h * Q:(h + 1) * Q, :rank] = (absorbed * scale).astype(BF16)
            turned = q_rope * qcos + swap_halves(q_rope) * qsin
            qf[h * Q:(h + 1) * Q, rank:] = (turned * scale).astype(BF16)

    halves = 2
    rr = R // halves

    def attend(keys, pos, key_dim):
        values = keys[:rank, :] if key_dim else keys[:, :rank]
        for g in range(halves):
            rows = pl.ds(g * rr, rr)
            s = lax.dot_general(
                qf[rows, :], keys, (((1,), (1 - key_dim,)), ((), ())), preferred_element_type=F32
            )
            s = jnp.where(pos < lim_s[rows, :], s, NEG)
            m_old = m_s[rows, :]
            m_new = jnp.maximum(m_old, jnp.max(s, axis=1, keepdims=True))
            p = jnp.exp(s - m_new)
            alpha = jnp.exp(m_old - m_new)
            m_s[rows, :] = m_new
            l_s[rows, :] = l_s[rows, :] * alpha + jnp.sum(p, axis=1, keepdims=True)
            acc_s[rows, :] = acc_s[rows, :] * alpha + lax.dot_general(
                p.astype(BF16), values, (((1,), (key_dim,)), ((), ())),
                preferred_element_type=F32,
            )

    def step(i, carry):
        c_kc(i).wait()
        pos = sq * (nb * bk) + i * bk + lax.broadcasted_iota(jnp.int32, (1, bk), 1)
        eff = pos
        for e in range(n_evicted):
            first = eb_ref[e] * BLK
            eff = jnp.where((pos >= first) & (pos < first + BLK), FAR, eff)
        attend(kc[i], eff, 1)
        return carry

    early = max(1, nb // 2)
    lax.fori_loop(0, early, step, 0)

    for d in range(1, T):
        rs_copy(d, near(d)).wait_recv()
    summed = rsum[0]
    for t in range(1, T):
        summed = summed + rsum[t]
    latent = summed[:, :rank]
    mean_square = jnp.mean(latent * latent, axis=-1, keepdims=True)
    normed = latent / jnp.sqrt(mean_square + NORM_EPS) * gain_ref[...].astype(F32).reshape(1, rank)
    tail = summed[:, rank:]
    turned = tail * rcos + swap_halves(tail) * rsin
    rown[:, :rank] = normed.astype(BF16)
    rown[:, rank:] = turned.astype(BF16)
    reb_ref[0] = rown[...]
    rall[me] = rown[...]
    for d in range(1, T):
        ag_copy(d, me).start()

    lax.fori_loop(early, nb, step, 0)

    for d in range(1, T):
        ag_copy(d, near(d)).wait_recv()
    fresh = jnp.concatenate([rall[t].astype(F32) for t in range(T)], axis=0).astype(BF16)
    flat = sq * half_rows + lax.broadcasted_iota(jnp.int32, (1, half_rows), 1)
    fpos = flat
    for e in range(n_evicted):
        inside = (flat >= e * BLK) & (flat < (e + 1) * BLK)
        fpos = jnp.where(inside, eb_ref[e] * BLK + flat - e * BLK, fpos)
    attend(fresh, fpos, 0)

    vh = wv.shape[2]
    gcols = (heads // ng) * vh

    def ex_copy(g):
        cols = pl.ds(g * gcols, gcols) if g < ng else pl.ds(heads * vh, 128)
        return pltpu.make_async_remote_copy(
            src_ref=osend.at[:, cols], dst_ref=orecv.at[:, cols], send_sem=ex_ss.at[g],
            recv_sem=ex_rs.at[g], device_id={"seq": other}, device_id_type=MESH,
        )

    lane = lax.broadcasted_iota(jnp.int32, (Q, 128), 1)
    stats = jnp.zeros((Q, 128), F32)
    for h in range(heads):
        stats = jnp.where(lane == h, m_s[h * Q:(h + 1) * Q, :], stats)
        stats = jnp.where(lane == heads + h, l_s[h * Q:(h + 1) * Q, :], stats)
    osend[:, heads * vh:] = stats
    ex_copy(ng).start()
    c_wv.wait()
    for g in range(ng):
        for h in range(g * (heads // ng), (g + 1) * (heads // ng)):
            a = acc_s[h * Q:(h + 1) * Q, :]
            high = a.astype(BF16)
            low = (a - high.astype(F32)).astype(BF16)
            both = jnp.dot(
                jnp.concatenate([high, low], axis=0), wv[h], preferred_element_type=F32
            )
            osend[:, h * vh:(h + 1) * vh] = both[:Q] + both[Q:]
        ex_copy(g).start()

    ex_copy(ng).wait_recv()
    theirs = orecv[:, heads * vh:]
    m_a, m_b = stats[:, :heads], theirs[:, :heads]
    joint = jnp.maximum(m_a, m_b)
    e_a, e_b = jnp.exp(m_a - joint), jnp.exp(m_b - joint)
    total = e_a * stats[:, heads:2 * heads] + e_b * theirs[:, heads:2 * heads]
    e_a, e_b = e_a / total, e_b / total
    for g in range(ng):
        ex_copy(g).wait_recv()
        for h in range(g * (heads // ng), (g + 1) * (heads // ng)):
            cols = slice(h * vh, (h + 1) * vh)
            att_ref[:, cols] = (
                e_a[:, h:h + 1] * osend[:, cols] + e_b[:, h:h + 1] * orecv[:, cols]
            ).astype(BF16)

    for d in range(1, T):
        ql_copy(d, me).wait_send()
        rs_copy(d, me).wait_send()
        ag_copy(d, me).wait_send()
    for g in range(ng + 1):
        ex_copy(g).wait_send()


def hand_over(reb_in, att_in, reb_out, att_out):
    reb_out[...] = reb_in[...]
    att_out[...] = att_in[...]


def body(
    stored_hidden, w_down_kv, kv_gain, evicted_blocks, query_latent, w_up_q,
    w_key_absorb, w_value, query_positions, prefix_lengths, latent_cache,
):
    T = lax.axis_size("tensor")
    rank = kv_gain.shape[0]
    heads, nope = w_key_absorb.shape[:2]
    width = w_down_kv.shape[1]
    rope_dim = width - rank
    Q = query_positions.shape[0]
    requests = prefix_lengths.shape[0]
    half_rows = stored_hidden.shape[1]
    local = half_rows // T
    cache_rows = latent_cache.shape[0]
    bk = min(2048, cache_rows)
    nb = cache_rows // bk
    nq = max(1, heads // 4)
    ng = max(1, heads // 4)
    vh = w_value.shape[2]
    R = heads * Q
    half = np.arange(rope_dim // 2, dtype=np.float64) * (-2.0 / rope_dim)
    freq = jnp.asarray(np.tile(10000.0 ** half, 2)[None, :].astype(np.float32))
    cfg = (T, heads, nope, rank, rope_dim, Q, requests, nq, nb, bk, ng)
    smem = pl.BlockSpec(memory_space=pltpu.SMEM)
    vmem = pl.BlockSpec(memory_space=pltpu.VMEM)
    hbm = pl.BlockSpec(memory_space=pl.ANY)
    dma = pltpu.SemaphoreType.DMA
    outs = pl.pallas_call(
        functools.partial(kernel, cfg),
        name="rebuild_attend",
        out_shape=(
            jax.ShapeDtypeStruct((1, local, width), BF16),
            jax.ShapeDtypeStruct((Q, heads * vh), BF16),
        ),
        in_specs=[smem] * 3 + [vmem] * 2 + [hbm] * 7,
        out_specs=(vmem, vmem),
        scratch_shapes=[
            pltpu.VMEM((half_rows, w_down_kv.shape[0]), BF16),
            pltpu.VMEM(w_down_kv.shape[::-1], BF16),
            pltpu.VMEM((T,) + query_latent.shape, BF16),
            pltpu.VMEM((Q, query_latent.shape[1]), F32),
            pltpu.VMEM(w_up_q.shape, BF16),
            pltpu.VMEM(w_key_absorb.shape, BF16),
            pltpu.VMEM(w_value.shape, BF16),
            pltpu.VMEM((nb, width, bk), BF16),
            pltpu.VMEM((R, width), BF16),
            pltpu.VMEM((T, local, width), F32),
            pltpu.VMEM((T, local, width), F32),
            pltpu.VMEM((local, width), BF16),
            pltpu.VMEM((T, local, width), BF16),
            pltpu.VMEM((R, 1), F32),
            pltpu.VMEM((R, 1), F32),
            pltpu.VMEM((R, rank), F32),
            pltpu.VMEM((R, 1), jnp.int32),
            pltpu.VMEM((Q, heads * vh + 128), F32),
            pltpu.VMEM((Q, heads * vh + 128), F32),
            dma((5,)), dma((nq,)), dma((nb,)),
            dma((T,)), dma((T,)), dma((T,)), dma((T,)), dma((T,)), dma((T,)),
            dma((ng + 1,)), dma((ng + 1,)),
        ],
        compiler_params=pltpu.CompilerParams(
            collective_id=0, has_side_effects=True, vmem_limit_bytes=60 * 1024 * 1024
        ),
    )(
        evicted_blocks, query_positions, prefix_lengths, freq, kv_gain,
        stored_hidden, w_down_kv.T, query_latent, w_up_q, w_key_absorb, w_value, latent_cache.T,
    )
    return pl.pallas_call(
        hand_over,
        name="hand_over",
        out_shape=tuple(jax.ShapeDtypeStruct(o.shape, o.dtype) for o in outs),
        in_specs=[vmem] * 2,
        out_specs=(vmem, vmem),
    )(*outs)


def solution(mesh):
    placed = (
        P(("groups", "seq"), None, "tensor"),
        P("tensor", None),
        P(),
        P("groups"),
        P(("groups", "tensor"), None),
        P(None, "tensor"),
        P("tensor", None, None),
        P("tensor", None, None),
        P("groups"),
        P("groups"),
        P(("groups", "seq"), None),
    )
    return jax.shard_map(
        body,
        mesh=mesh,
        in_specs=placed,
        out_specs=(P(("groups", "seq"), "tensor", None), P("groups", "tensor")),
        check_vma=False,
    )
```
